256 devices in a mesh: group: 16 (over y_hi, z), member: 16 (over y_lo, x, core).
Axes of the slice: x: 4, y: 4 (y_hi: 2, y_lo: 2; y = y_hi * 2 + y_lo), z: 8, core: 2. Of those that a mesh axis runs over, the one named last changes fastest.
Arguments:
- points: float32 [256, 8, 1024], P(('group', 'member')), may hold values from -4 to 4
- inverse_cov: bfloat16 [256, 1024, 1024], P(('group', 'member')), may hold values from -1 to 4, as said below
- targets: bfloat16 [256, 1024], P(('group', 'member')), may hold values from -6 to 6
- queries: float32 [8, 4096], P(None, ('group', 'member')), may hold values from -4 to 4
- prior_precision: float32 [4096], P(('group', 'member')), may hold values from 0.05 to 0.2
- batch_order: int32 [4096], replicated, may hold values from 0 to 4095, each once
- noise: float32 [4096, 4096], P('group', 'member'), may hold values from -6 to 6
Outputs:
- samples: float32 [4096, 4096], P('group', 'member')
The draws below stay inside these ranges and needn't reach their ends.
Inputs may be any that keep to these rules, and one draw needn't show every extreme that they name: `batch_order`: each query number appears exactly once. `inverse_cov`: each expert's matrix is symmetric positive definite.
All inputs are finite; a program needn't handle non-finite values.
Results may differ from the reference program's by a relative error of at most 0.0025.
Values sent between devices are 32-bit elements; how exact they have to be, the bound alone decides.
No kernel may reach another device: no remote copies, remote signals or barrier semaphores. Data moves between devices by JAX's collectives and lax.ppermute only.
A program may use at most 128 MiB of HBM per device.

```python
import math
import jax
import jax.numpy as jnp
from jax import lax

DIM = 8
M = 1024
QB = 256
EXPERTS = 256
QUERIES = 4096
SAMPLES = 4096


def draw_points(key, part):
    base = jax.random.normal(jax.random.fold_in(key, 32), (EXPERTS, DIM, M), jnp.float32)
    return jnp.clip(base, -2.5, 2.5) * 1.6


def draw_queries(key, part):
    base = jax.random.normal(jax.random.fold_in(key, 34), (DIM, QUERIES), jnp.float32)
    return jnp.clip(base, -2.5, 2.5) * 1.6


def draw_inverse_cov(key, part):
    base = jax.random.normal(jax.random.fold_in(key, 11), (EXPERTS, M, M), jnp.float32)
    spread = 0.25 / M ** 0.5
    offdiag = (base + jnp.swapaxes(base, 1, 2)) * (spread / 2.0 ** 0.5)
    matrix = offdiag + jnp.eye(M, dtype=jnp.float32)[None, :, :]
    return matrix.astype(jnp.bfloat16)


def block_levels(own_key, shape, shards, smallest, top_value):
    factor_of, own = 1.0, jax.random.fold_in(own_key, 6)
    for axis_at, blocks in shards:
        draws = jnp.exp(jax.random.uniform(jax.random.fold_in(own, axis_at), (blocks,), jnp.float32, smallest / len(shards), top_value / len(shards)))
        factor_of = factor_of * jnp.repeat(draws, shape[axis_at] // blocks).reshape([-1 if axis == axis_at else 1 for axis in range(len(shape))])
    return factor_of


def normal_values(key, shape, width, most, cuts=(), kind=jnp.bfloat16):
    array = jax.random.normal(key, shape, jnp.float32) * width
    if len(cuts) > 0:
        array = block_levels(key, shape, cuts, -0.22, 0.18) * array
    return jnp.clip(array, min=-most, max=most).astype(kind)


def setup_inputs(seed: int = 0) -> dict:
    arg_keys = jax.random.split(jax.random.key(seed), 8)
    return {
        "points": draw_points(jax.random.fold_in(arg_keys[7], 71), 0),
        "inverse_cov": draw_inverse_cov(jax.random.fold_in(arg_keys[7], 71), 0),
        "targets": normal_values(arg_keys[2], (EXPERTS, M), 1.0, 6.0, ((0, 256),)),
        "queries": draw_queries(jax.random.fold_in(arg_keys[7], 71), 0),
        "prior_precision": jnp.clip(jnp.exp(math.log(0.2) - 1.3862944 * jax.random.uniform(arg_keys[4], (QUERIES,), jnp.float32) ** block_levels(arg_keys[4], (QUERIES,), ((0, 256),), -0.2, 0.2)), 0.05, 0.2),
        "batch_order": jax.random.permutation(arg_keys[5], QUERIES).astype(jnp.int32),
        "noise": normal_values(arg_keys[6], (QUERIES, SAMPLES), 1.0, 6.0, ((0, 16), (1, 16)), jnp.float32),
    }


kernel_rate = 0.25

def kernel_rows(ordered, coords):
    inner = jnp.dot(ordered.T.astype(jnp.float32), coords.astype(jnp.float32), precision=lax.Precision.HIGHEST, preferred_element_type=jnp.float32)
    dist = jnp.sum(ordered * ordered, axis=0)[:, None] + jnp.sum(coords * coords, axis=0)[None, :] - 2.0 * inner
    return jnp.exp(-kernel_rate * dist).astype(jnp.bfloat16)

def reference(points, inverse_cov, targets, queries, prior_precision, batch_order, noise):
    batches = QUERIES // QB
    ordered = jnp.take(queries, batch_order, axis=1)
    prior_sorted = jnp.take(prior_precision, batch_order)

    def step(carry, expert):
        precision, info = carry
        coords, inverse, values = expert
        cross = kernel_rows(ordered, coords)
        proj = jnp.dot(cross.astype(jnp.float32), inverse.astype(jnp.float32), preferred_element_type=jnp.float32).astype(jnp.bfloat16)
        info = info + jnp.dot(proj.astype(jnp.float32), values.astype(jnp.float32), preferred_element_type=jnp.float32)
        precision = precision + jnp.einsum('bqm,bpm->bqp', proj.reshape(batches, QB, M).astype(jnp.float32), cross.reshape(batches, QB, M).astype(jnp.float32), precision=lax.Precision.HIGHEST)
        return ((precision, info), None)
    start = (jnp.zeros((batches, QB, QB), jnp.float32), jnp.zeros((QUERIES,), jnp.float32))
    (precision, info), _ = lax.scan(step, start, (points, inverse_cov, targets))
    precision = precision / EXPERTS + prior_sorted.reshape(batches, QB)[:, :, None] * jnp.eye(QB, dtype=jnp.float32)
    info = (info / EXPERTS).reshape(batches, QB, 1)
    factor = jnp.linalg.cholesky(precision)
    forward = lax.linalg.triangular_solve(factor, info, left_side=True, lower=True)
    right_side = forward + noise.reshape(batches, QB, SAMPLES)
    result = lax.linalg.triangular_solve(factor, right_side, left_side=True, lower=True, transpose_a=True)
    return result.reshape(QUERIES, SAMPLES)
```

```python
import jax
import jax.numpy as jnp
from jax import lax
from jax.experimental import pallas as pl
from jax.experimental.pallas import tpu as pltpu
from jax.sharding import Mesh
from jax.sharding import PartitionSpec as P

AXES = ("yh", "z", "yl", "x", "c")
GROUP = ("yh", "z")
MEMBER = ("yl", "x", "c")
RATE = 0.25
F32, BF16 = jnp.float32, jnp.bfloat16


def iota(shape, dim):
    return lax.broadcasted_iota(jnp.int32, shape, dim)


def dot(a, b, dims):
    return lax.dot_general(a, b, (dims, ((), ())), preferred_element_type=F32)


def three_parts(v):
    a = v.astype(BF16).astype(F32)
    b = (v - a).astype(BF16).astype(F32)
    return a, b, (v - a - b)


def expert_kernel(me_ref, order_ref, table_ref, points_ref, inv_ref, targets_ref,
                  own_ref, other_ref, parts_s, fold_s, points_s, cross_s):
    b = pl.program_id(0)

    @pl.when(b == 0)
    def _():
        table = table_ref[:, 0:128].T
        parts_s[...] = jnp.concatenate(three_parts(table), axis=0).astype(BF16)
        fold_s[...] = (iota((32, 384), 1) // 16 == iota((32, 384), 0)).astype(F32).astype(BF16)
        p = points_ref[0]
        norm = -RATE * jnp.sum(p * p, axis=0, keepdims=True)
        h, m, l = three_parts(2.0 * RATE * p)
        one = jnp.ones((3, p.shape[1]), F32)
        tail = jnp.concatenate([one, *three_parts(norm), jnp.zeros((2, p.shape[1]), F32)], axis=0)
        points_s[...] = jnp.concatenate([h, m, l, h, m, l, h, m, l, tail], axis=0).astype(BF16)
        cross_s[256:272, :] = jnp.where(
            iota((16, 1024), 0) == 0, jnp.broadcast_to(targets_ref[...].astype(F32), (16, 1024)), 0.0
        ).astype(BF16)

    o = order_ref[pl.ds(b, 1), :]
    hi = lax.shift_right_logical(o, 4)
    row = (hi & 128) | ((hi & 7) << 4) | (lax.shift_right_logical(hi, 3) & 15)
    hot = jnp.where(iota((256, 256), 0) == row, 1.0, 0.0).astype(BF16)
    picked = dot(parts_s[...], hot, ((1,), (0,)))
    picked = jnp.where((iota((384, 256), 0) & 15) == (o & 15), picked, 0.0).astype(BF16)
    q = dot(fold_s[...], picked, ((1,), (0,)))
    h, m, l = q[0:8], q[8:16], q[16:24]
    full = (h + m) + l
    norm = -RATE * jnp.sum(full * full, axis=0, keepdims=True)
    tail = jnp.concatenate([*three_parts(norm), jnp.ones((3, 256), F32), jnp.zeros((2, 256), F32)], axis=0)
    left = jnp.concatenate([h, h, h, m, m, m, l, l, l, tail], axis=0).T.astype(BF16)
    power = dot(left, points_s[...], ((1,), (0,)))
    cross_s[0:256, :] = jnp.exp(power).astype(BF16)
    proj = dot(cross_s[0:256, :], inv_ref[0], ((1,), (0,))).astype(BF16)
    terms = dot(cross_s[...], proj, ((1,), (1,)))
    low = iota((128, 128), 0) - iota((128, 128), 1)
    first = terms[0:128, 0:128]
    mixed = jnp.where(low > 0, first, terms[128:256, 128:256])
    diag = jnp.sum(jnp.where(low == 0, first, 0.0), axis=0, keepdims=True)
    info = terms[256:257, :]
    extra = jnp.concatenate([diag, info[:, 0:128], info[:, 128:256], jnp.zeros((13, 128), F32)], axis=0)
    core = me_ref[0]
    start = (b // 8) * 1088 + (b % 8) * 17
    for r in range(17):
        if r < 8:
            rows = terms[128 + 16 * r : 144 + 16 * r, 0:128]
        elif r < 16:
            rows = mixed[16 * (r - 8) : 16 * (r - 7), :]
        else:
            rows = extra
        a, c = rows[0:8], rows[8:16]
        own_ref[pl.ds(start + r, 8, stride=136), :] = jnp.where(core == 0, a, c)
        other_ref[pl.ds(start + r, 8, stride=136), :] = jnp.where(core == 0, c, a)


def expert_terms(core, order, table, points, inverse_cov, targets):
    whole = lambda *shape: pl.BlockSpec(shape, lambda b, me: (0,) * len(shape))
    return pl.pallas_call(
        expert_kernel,
        out_shape=(jax.ShapeDtypeStruct((2176, 128), F32),) * 2,
        grid_spec=pltpu.PrefetchScalarGridSpec(
            num_scalar_prefetch=1,
            grid=(16,),
            in_specs=[whole(16, 256), whole(256, 144), whole(1, 8, 1024), whole(1, 1024, 1024), whole(1, 1024)],
            out_specs=(whole(2176, 128),) * 2,
            scratch_shapes=[
                pltpu.VMEM((384, 256), BF16),
                pltpu.VMEM((32, 384), BF16),
                pltpu.VMEM((80, 1024), BF16),
                pltpu.VMEM((272, 1024), BF16),
            ],
        ),
        compiler_params=pltpu.CompilerParams(
            dimension_semantics=("arbitrary",), vmem_limit_bytes=40 << 20
        ),
        name="expert",
    )(core, order, table, points, inverse_cov, targets)


def from_everyone(v, axes, n):
    return lax.all_to_all(jnp.broadcast_to(v[None], (n, *v.shape)), axes, 0, 0, tiled=True)


def per_device(points, inverse_cov, targets, queries, prior_precision, batch_order, noise):
    mine = jnp.concatenate([queries.reshape(-1), prior_precision])
    table = from_everyone(mine, ("z", "yl"), 16)
    table = from_everyone(table, ("yh", "x", "c"), 16).reshape(256, 144)
    order = batch_order.reshape(16, 256)
    core = lax.axis_index("c")
    own, other = expert_terms(core[None], order, table, points, inverse_cov, targets)
    own = own + lax.ppermute(other, "c", [(0, 1), (1, 0)])
    part = lax.all_to_all(own.reshape(16, 136, 128), ("yh", "x", "yl"), 0, 0, tiled=True).sum(0)
    part = part.reshape(8, 1, 17 * 128)
    part = jnp.broadcast_to(part, (8, 2, 17 * 128)).reshape(16, 17 * 128)
    part = lax.all_to_all(part, ("z", "yl"), 0, 0, tiled=True).reshape(8, 2 * 17 * 128).sum(0)
    pieces = from_everyone(part, ("c", "x"), 8).reshape(16, 17, 128)

    packed = jnp.moveaxis(pieces, 0, 1).reshape(272, 128) / 256.0
    mixed = packed[128:256]
    first = jnp.tril(mixed, -1) + jnp.diag(packed[256]) + jnp.tril(mixed, -1).T
    second = jnp.triu(mixed) + jnp.triu(mixed, 1).T
    corner = packed[0:128]
    precision = jnp.block([[first, corner.T], [corner, second]])
    info = packed[257:259].reshape(256, 1)
    group = lax.axis_index(GROUP)
    o = lax.dynamic_index_in_dim(order, group, 0, keepdims=False)
    hi = o >> 4
    row = (hi & 128) | ((hi & 7) << 4) | ((hi >> 3) & 15)
    prior = table[:, 128:][row, o & 15]
    precision = precision + jnp.diag(prior)
    factor = jnp.linalg.cholesky(precision)
    forward = lax.linalg.triangular_solve(factor, info, left_side=True, lower=True)
    return lax.linalg.triangular_solve(
        factor, forward + noise, left_side=True, lower=True, transpose_a=True
    )


def solution(mesh):
    finer = Mesh(mesh.devices.reshape(2, 8, 2, 4, 2), AXES)
    in_specs = (
        P(AXES, None, None),
        P(AXES, None, None),
        P(AXES, None),
        P(None, AXES),
        P(AXES),
        P(),
        P(GROUP, MEMBER),
    )
    return jax.shard_map(
        per_device, mesh=finer, in_specs=in_specs, out_specs=P(GROUP, MEMBER), check_vma=False
    )
```

```python
import jax
import jax.numpy as jnp
from jax import lax
from jax.experimental import pallas as pl
from jax.experimental.pallas import tpu as pltpu
from jax.sharding import Mesh
from jax.sharding import PartitionSpec as P

AXES = ("yh", "z", "yl", "x", "c")
GROUP = ("yh", "z")
MEMBER = ("yl", "x", "c")
RATE = 0.25
F32, BF16 = jnp.float32, jnp.bfloat16


def iota(shape, dim):
    return lax.broadcasted_iota(jnp.int32, shape, dim)


def dot(a, b, dims):
    return lax.dot_general(a, b, (dims, ((), ())), preferred_element_type=F32)


def three_parts(v):
    a = v.astype(BF16).astype(F32)
    b = (v - a).astype(BF16).astype(F32)
    return a, b, (v - a - b)


def expert_kernel(me_ref, order_ref, table_ref, points_ref, inv_ref, targets_ref,
                  own_ref, other_ref, parts_s, fold_s, points_s, cross_s):
    b = pl.program_id(0)

    @pl.when(b == 0)
    def _():
        parts_s[0:384, :] = jnp.concatenate(three_parts(table_ref[:, 0:128].T), axis=0).astype(BF16)
        parts_s[384:432, :] = jnp.concatenate(three_parts(table_ref[:, 128:144].T), axis=0).astype(BF16)
        fold_s[...] = (iota((32, 432), 1) // 16 == iota((32, 432), 0)).astype(F32).astype(BF16)
        p = points_ref[0]
        norm = -RATE * jnp.sum(p * p, axis=0, keepdims=True)
        h, m, l = three_parts(2.0 * RATE * p)
        one = jnp.ones((3, p.shape[1]), F32)
        tail = jnp.concatenate([one, *three_parts(norm), jnp.zeros((2, p.shape[1]), F32)], axis=0)
        points_s[...] = jnp.concatenate([h, m, l, h, m, l, h, m, l, tail], axis=0).astype(BF16)
        cross_s[256:272, :] = jnp.where(
            iota((16, 1024), 0) == 0, jnp.broadcast_to(targets_ref[...].astype(F32), (16, 1024)), 0.0
        ).astype(BF16)

    o = order_ref[pl.ds(b, 1), :]
    hi = lax.shift_right_logical(o, 4)
    row = (hi & 128) | ((hi & 7) << 4) | (lax.shift_right_logical(hi, 3) & 15)
    hot = jnp.where(iota((256, 256), 0) == row, 1.0, 0.0).astype(BF16)
    picked = dot(parts_s[...], hot, ((1,), (0,)))
    picked = jnp.where((iota((432, 256), 0) & 15) == (o & 15), picked, 0.0).astype(BF16)
    q = dot(fold_s[...], picked, ((1,), (0,)))
    h, m, l = q[0:8], q[8:16], q[16:24]
    full = (h + m) + l
    prior = (q[24:25] + q[25:26]) + q[26:27]
    norm = -RATE * jnp.sum(full * full, axis=0, keepdims=True)
    tail = jnp.concatenate([*three_parts(norm), jnp.ones((3, 256), F32), jnp.zeros((2, 256), F32)], axis=0)
    left = jnp.concatenate([h, h, h, m, m, m, l, l, l, tail], axis=0).T.astype(BF16)
    power = dot(left, points_s[...], ((1,), (0,)))
    cross_s[0:256, :] = jnp.exp(power).astype(BF16)
    proj = dot(cross_s[0:256, :], inv_ref[0], ((1,), (0,))).astype(BF16)
    terms = dot(cross_s[...], proj, ((1,), (1,)))
    low = iota((128, 128), 0) - iota((128, 128), 1)
    first = terms[0:128, 0:128]
    second = terms[128:256, 128:256] + jnp.where(low == 0, prior[:, 128:256], 0.0)
    mixed = jnp.where(low > 0, first, second)
    diag = jnp.sum(jnp.where(low == 0, first, 0.0), axis=0, keepdims=True) + prior[:, 0:128]
    info = terms[256:257, :]
    extra = jnp.concatenate([diag, info[:, 0:128], info[:, 128:256], jnp.zeros((13, 128), F32)], axis=0)
    core = me_ref[0]
    start = (b // 8) * 1088 + (b % 8) * 17
    for r in range(17):
        if r < 8:
            rows = terms[128 + 16 * r : 144 + 16 * r, 0:128]
        elif r < 16:
            rows = mixed[16 * (r - 8) : 16 * (r - 7), :]
        else:
            rows = extra
        a, c = rows[0:8], rows[8:16]
        own_ref[pl.ds(start + r, 8, stride=136), :] = jnp.where(core == 0, a, c)
        other_ref[pl.ds(start + r, 8, stride=136), :] = jnp.where(core == 0, c, a)


def expert_terms(core, order, table, points, inverse_cov, targets):
    whole = lambda *shape: pl.BlockSpec(shape, lambda b, me: (0,) * len(shape))
    return pl.pallas_call(
        expert_kernel,
        out_shape=(jax.ShapeDtypeStruct((2176, 128), F32),) * 2,
        grid_spec=pltpu.PrefetchScalarGridSpec(
            num_scalar_prefetch=1,
            grid=(16,),
            in_specs=[whole(16, 256), whole(256, 144), whole(1, 8, 1024), whole(1, 1024, 1024), whole(1, 1024)],
            out_specs=(whole(2176, 128),) * 2,
            scratch_shapes=[
                pltpu.VMEM((432, 256), BF16),
                pltpu.VMEM((32, 432), BF16),
                pltpu.VMEM((80, 1024), BF16),
                pltpu.VMEM((272, 1024), BF16),
            ],
        ),
        compiler_params=pltpu.CompilerParams(
            dimension_semantics=("arbitrary",), vmem_limit_bytes=40 << 20
        ),
        name="expert",
    )(core, order, table, points, inverse_cov, targets)


def exact_dot(a, b, dims):
    return lax.dot_general(
        a, b, (dims, ((), ())), precision=lax.Precision.HIGHEST, preferred_element_type=F32
    )


def along_lanes(v, i):
    return jnp.broadcast_to(v[:, i : i + 1], (8, 128))


def along_rows(v, i):
    return jnp.broadcast_to(v[i : i + 1, :], (8, 128))


def factor_block(groups, done_ref):
    for p in range(8):
        g = groups[p]
        cols = [along_lanes(g, 8 * p + j) for j in range(8)]
        b = [[along_rows(cols[j], i) for j in range(i + 1)] for i in range(8)]
        rows = [along_rows(g, i) for i in range(8)]
        ahead = [[along_lanes(groups[t], 8 * p + j) for j in range(8)] for t in range(p + 1, 8)]
        for k in range(8):
            r = lax.rsqrt(b[k][k])
            for i in range(k + 1, 8):
                b[i][k] = b[i][k] * r
            for i in range(k + 1, 8):
                for j in range(k + 1, i + 1):
                    b[i][j] = b[i][j] - b[i][k] * b[j][k]
            rows[k] = rows[k] * r
            for i in range(k + 1, 8):
                rows[i] = rows[i] - b[i][k] * rows[k]
            for t in range(p + 1, 8):
                c = ahead[t - p - 1]
                c[k] = c[k] * r
                for j in range(k + 1, 8):
                    c[j] = c[j] - c[k] * b[j][k]
                groups[t] = groups[t] - c[k] * rows[k]
            done_ref[8 * p + k : 8 * p + k + 1, :] = rows[k][0:1]


def solve_kernel(pieces_ref, noise_ref, out_ref, aug_s, done_s, inverse_s):
    scale = 1.0 / 256.0

    def packed(r):
        return jnp.concatenate(
            [pieces_ref[pl.ds(r, 8, stride=17), :], pieces_ref[pl.ds(136 + r, 8, stride=17), :]], axis=0
        ) * scale

    corner = jnp.concatenate([packed(r) for r in range(8)], axis=0)
    mixed = jnp.concatenate([packed(r) for r in range(8, 16)], axis=0)
    extra = packed(16)
    flipped = mixed.T
    low = iota((128, 128), 0) - iota((128, 128), 1)
    first = jnp.where(low > 0, mixed, jnp.where(low < 0, flipped, jnp.broadcast_to(extra[0:1], (128, 128))))
    second = jnp.where(low > 0, flipped, mixed)
    aug_s[0:128, 0:128] = first
    aug_s[0:128, 128:256] = corner.T
    aug_s[128:256, 0:128] = corner
    aug_s[128:256, 128:256] = second
    aug_s[:, 256:512] = jnp.where(iota((256, 256), 0) == iota((256, 256), 1), 1.0, 0.0)
    inverse_s[...] = jnp.zeros((256, 256), F32)
    lane = iota((64, 128), 1)
    unit = jnp.where(iota((64, 128), 0) + 64 == lane, 1.0, 0.0)
    for s in range(4):
        top, tile = 64 * s, 128 * (s // 2)
        block = aug_s[top : top + 64, tile : tile + 128]
        if s % 2:
            block = pltpu.roll(block, 64, 1)
        block = jnp.where(lane < 64, block, unit)
        factor_block([block[8 * t : 8 * t + 8] for t in range(8)], done_s)
        inv = pltpu.roll(done_s[...], 64, 1)[:, 0:64]
        wide = 128 * (s // 2 + 1)
        inverse = exact_dot(inv, aug_s[top : top + 64, 256 : 256 + wide], ((1,), (0,)))
        inverse_s[top : top + 64, 0:wide] = inverse
        if s < 3:
            begin = 128 * ((s + 1) // 2)
            upper = exact_dot(inv, aug_s[top : top + 64, begin:256], ((1,), (0,)))
            lower = upper.T[top + 64 - begin :]
            rest = slice(top + 64, 256)
            aug_s[rest, begin:256] = aug_s[rest, begin:256] - exact_dot(lower, upper, ((1,), (0,)))
            aug_s[rest, 256 : 256 + wide] = aug_s[rest, 256 : 256 + wide] - exact_dot(
                lower, inverse, ((1,), (0,))
            )
    info = jnp.concatenate([extra[1:2], extra[2:3]], axis=1)
    inverse = inverse_s[...]
    forward = jnp.sum(inverse * info, axis=1, keepdims=True)
    out_ref[...] = exact_dot(inverse.T, noise_ref[...] + forward, ((1,), (0,)))


def draw_samples(pieces, noise):
    return pl.pallas_call(
        solve_kernel,
        out_shape=jax.ShapeDtypeStruct((256, 256), F32),
        scratch_shapes=[
            pltpu.VMEM((256, 512), F32),
            pltpu.VMEM((64, 128), F32),
            pltpu.VMEM((256, 256), F32),
        ],
        name="solve",
    )(pieces, noise)


def from_everyone(v, axes, n):
    return lax.all_to_all(jnp.broadcast_to(v[None], (n, *v.shape)), axes, 0, 0, tiled=True)


def per_device(points, inverse_cov, targets, queries, prior_precision, batch_order, noise):
    mine = jnp.concatenate([queries.reshape(-1), prior_precision])
    table = from_everyone(mine, ("z", "yl"), 16)
    table = from_everyone(table, ("yh", "x", "c"), 16).reshape(256, 144)
    order = batch_order.reshape(16, 256)
    core = lax.axis_index("c")
    own, other = expert_terms(core[None], order, table, points, inverse_cov, targets)
    own = own + lax.ppermute(other, "c", [(0, 1), (1, 0)])
    part = lax.all_to_all(own.reshape(16, 136, 128), ("yh", "x", "yl"), 0, 0, tiled=True).sum(0)
    part = part.reshape(8, 1, 17 * 128)
    part = jnp.broadcast_to(part, (8, 2, 17 * 128)).reshape(16, 17 * 128)
    part = lax.all_to_all(part, ("z", "yl"), 0, 0, tiled=True).reshape(8, 2 * 17 * 128).sum(0)
    pieces = from_everyone(part, ("c", "x"), 8).reshape(272, 128)
    return draw_samples(pieces, noise)


def solution(mesh):
    finer = Mesh(mesh.devices.reshape(2, 8, 2, 4, 2), AXES)
    in_specs = (
        P(AXES, None, None),
        P(AXES, None, None),
        P(AXES, None),
        P(None, AXES),
        P(AXES),
        P(),
        P(GROUP, MEMBER),
    )
    return jax.shard_map(
        per_device, mesh=finer, in_specs=in_specs, out_specs=P(GROUP, MEMBER), check_vma=False
    )
```

```python
import jax
import jax.numpy as jnp
from jax import lax
from jax.experimental import pallas as pl
from jax.experimental.pallas import tpu as pltpu
from jax.sharding import Mesh
from jax.sharding import PartitionSpec as P

AXES = ("yh", "z", "yl", "x", "c")
GROUP = ("yh", "z")
MEMBER = ("yl", "x", "c")
RATE = 0.25
EXPERT_VMEM = 60 << 20
F32, BF16 = jnp.float32, jnp.bfloat16


def iota(shape, dim):
    return lax.broadcasted_iota(jnp.int32, shape, dim)


def dot(a, b, dims):
    return lax.dot_general(a, b, (dims, ((), ())), preferred_element_type=F32)


def three_parts(v):
    a = v.astype(BF16).astype(F32)
    b = (v - a).astype(BF16).astype(F32)
    return a, b, (v - a - b)


def expert_kernel(me_ref, order_ref, table_ref, points_hbm, inv_hbm, targets_hbm, own_ref, other_ref,
                  parts_s, fold_s, points_s, cross0_s, cross1_s, proj0_s, proj1_s, left_s, prior_s,
                  inv_s, raw_s, target_s, sem):
    copies = [
        pltpu.make_async_copy(inv_hbm.at[0], inv_s, sem.at[0]),
        pltpu.make_async_copy(points_hbm.at[0], raw_s, sem.at[1]),
        pltpu.make_async_copy(targets_hbm, target_s, sem.at[2]),
    ]
    for c in copies:
        c.start()
    core = me_ref[0]
    cross, proj = (cross0_s, cross1_s), (proj0_s, proj1_s)

    def pick(n, carry):
        o = order_ref[pl.ds(pl.multiple_of(n * 1024, 1024), 1024)].reshape(1, 1024)
        hi = lax.shift_right_logical(o, 4)
        row = (hi & 128) | ((hi & 14) << 3) | (lax.shift_right_logical(hi, 3) & 14) | (hi & 1)
        hot = jnp.where(iota((256, 1024), 0) == row, 1.0, 0.0).astype(BF16)
        picked = dot(parts_s[...], hot, ((1,), (0,)))
        picked = jnp.where((iota((432, 1024), 0) & 15) == (o & 15), picked, 0.0).astype(BF16)
        q = dot(fold_s[...], picked, ((1,), (0,)))
        h, m, l = q[0:8], q[8:16], q[16:24]
        full = (h + m) + l
        norm = -RATE * jnp.sum(full * full, axis=0, keepdims=True)
        tail = jnp.concatenate([*three_parts(norm), jnp.ones((3, 1024), F32), jnp.zeros((2, 1024), F32)], axis=0)
        stacked = jnp.concatenate([h, h, h, m, m, m, l, l, l, tail], axis=0)
        left_s[pl.ds(pl.multiple_of(n * 1024, 1024), 1024), :] = stacked.T.astype(BF16)
        prior_s[pl.ds(n, 1), :] = (q[24:25] + q[25:26]) + q[26:27]
        return carry

    def kernel_columns(b, slot, j):
        at = slice(256 * j, 256 * j + 256)
        for k in range(2):
            rows = left_s[pl.ds(pl.multiple_of((b + k) * 256, 256), 256), :]
            power = dot(rows, points_s[:, at], ((1,), (0,)))
            cross[slot][272 * k : 272 * k + 256, at] = jnp.exp(power).astype(BF16)

    def write(b, terms, info, prior):
        low = iota((128, 128), 0) - iota((128, 128), 1)
        first = terms[0:128, 0:128]
        second = terms[128:256, 128:256] + jnp.where(low == 0, prior[:, 128:256], 0.0)
        mixed = jnp.where(low > 0, first, second)
        diag = jnp.sum(jnp.where(low == 0, first, 0.0), axis=0, keepdims=True) + prior[:, 0:128]
        extra = jnp.concatenate([diag, info[:, 0:128], info[:, 128:256], jnp.zeros((13, 128), F32)], axis=0)
        start = (b // 8) * 1088 + (b % 8) * 17
        for r in range(17):
            if r < 8:
                rows = terms[128 + 16 * r : 144 + 16 * r, 0:128]
            elif r < 16:
                rows = mixed[16 * (r - 8) : 16 * (r - 7), :]
            else:
                rows = extra
            a, c = rows[0:8], rows[8:16]
            own_ref[pl.ds(start + r, 8, stride=136), :] = jnp.where(core == 0, a, c)
            other_ref[pl.ds(start + r, 8, stride=136), :] = jnp.where(core == 0, c, a)

    def precision(b, slot):
        for k in range(2):
            terms = dot(
                cross[slot][256 * k : 256 * k + 272, :], proj[slot][272 * k : 272 * k + 256, :], ((1,), (1,))
            )
            prior = prior_s[pl.ds(b // 4, 1), :]
            at = 512 * slot + 256 * k
            info = terms[256:257] if k == 0 else terms[0:1]
            write(b + k, terms[16 * k : 16 * k + 256], info, prior[:, at : at + 256])

    def main(b, slot, before, after):
        for j in range(4):
            at = slice(256 * j, 256 * j + 256)
            proj[slot][:, at] = dot(cross[slot][...], inv_s[:, at], ((1,), (0,))).astype(BF16)
            if j == 0:
                precision(before, 1 - slot)
            kernel_columns(after, 1 - slot, j)

    parts_s[0:384, :] = jnp.concatenate(three_parts(table_ref[:, 0:128].T), axis=0).astype(BF16)
    parts_s[384:432, :] = jnp.concatenate(three_parts(table_ref[:, 128:144].T), axis=0).astype(BF16)
    fold_s[...] = (iota((32, 432), 1) // 16 == iota((32, 432), 0)).astype(F32).astype(BF16)
    lax.fori_loop(0, 4, pick, 0)
    copies[1].wait()
    p = raw_s[...]
    norm = -RATE * jnp.sum(p * p, axis=0, keepdims=True)
    h, m, l = three_parts(2.0 * RATE * p)
    one = jnp.ones((3, p.shape[1]), F32)
    tail = jnp.concatenate([one, *three_parts(norm), jnp.zeros((2, p.shape[1]), F32)], axis=0)
    points_s[...] = jnp.concatenate([h, m, l, h, m, l, h, m, l, tail], axis=0).astype(BF16)
    copies[2].wait()
    goal = jnp.where(
        iota((16, 1024), 0) == 0, jnp.broadcast_to(target_s[...].astype(F32), (16, 1024)), 0.0
    ).astype(BF16)
    cross0_s[256:272, :] = goal
    cross1_s[256:272, :] = goal
    for j in range(4):
        kernel_columns(0, 0, j)
    copies[0].wait()

    def step(i, carry):
        b = 4 * i
        main(b, 0, jnp.maximum(b - 2, 0), b + 2)
        main(b + 2, 1, b, jnp.minimum(b + 4, 14))
        return carry

    lax.fori_loop(0, 4, step, 0)
    precision(14, 1)


def expert_terms(core, order, table, points, inverse_cov, targets):
    vmem = pl.BlockSpec(memory_space=pltpu.VMEM)
    hbm = pl.BlockSpec(memory_space=pltpu.HBM)
    return pl.pallas_call(
        expert_kernel,
        out_shape=(jax.ShapeDtypeStruct((2176, 128), F32),) * 2,
        in_specs=[pl.BlockSpec(memory_space=pltpu.SMEM), vmem, vmem, hbm, hbm, hbm],
        out_specs=(vmem, vmem),
        scratch_shapes=[
            pltpu.VMEM((432, 256), BF16),
            pltpu.VMEM((32, 432), BF16),
            pltpu.VMEM((80, 1024), BF16),
            pltpu.VMEM((528, 1024), BF16),
            pltpu.VMEM((528, 1024), BF16),
            pltpu.VMEM((528, 1024), BF16),
            pltpu.VMEM((528, 1024), BF16),
            pltpu.VMEM((4096, 80), BF16),
            pltpu.VMEM((8, 1024), F32),
            pltpu.VMEM((1024, 1024), BF16),
            pltpu.VMEM((8, 1024), F32),
            pltpu.VMEM((1, 1024), BF16),
            pltpu.SemaphoreType.DMA((3,)),
        ],
        compiler_params=pltpu.CompilerParams(vmem_limit_bytes=EXPERT_VMEM),
        name="expert",
    )(core, order, table, points, inverse_cov, targets)


def exact_dot(a, b, dims):
    return lax.dot_general(
        a, b, (dims, ((), ())), precision=lax.Precision.HIGHEST, preferred_element_type=F32
    )


def along_lanes(v, i):
    return jnp.broadcast_to(v[:, i : i + 1], (8, 128))


def along_rows(v, i):
    return jnp.broadcast_to(v[i : i + 1, :], (8, 128))


def factor_block(groups, done_ref):
    for p in range(8):
        g = groups[p]
        cols = [along_lanes(g, 8 * p + j) for j in range(8)]
        b = [[along_rows(cols[j], i) for j in range(i + 1)] for i in range(8)]
        rows = [along_rows(g, i) for i in range(8)]
        ahead = [[along_lanes(groups[t], 8 * p + j) for j in range(8)] for t in range(p + 1, 8)]
        for k in range(8):
            r = lax.rsqrt(b[k][k])
            for i in range(k + 1, 8):
                b[i][k] = b[i][k] * r
            for i in range(k + 1, 8):
                for j in range(k + 1, i + 1):
                    b[i][j] = b[i][j] - b[i][k] * b[j][k]
            rows[k] = rows[k] * r
            for i in range(k + 1, 8):
                rows[i] = rows[i] - b[i][k] * rows[k]
            for t in range(p + 1, 8):
                c = ahead[t - p - 1]
                c[k] = c[k] * r
                for j in range(k + 1, 8):
                    c[j] = c[j] - c[k] * b[j][k]
                groups[t] = groups[t] - c[k] * rows[k]
            done_ref[8 * p + k : 8 * p + k + 1, :] = rows[k][0:1]


def solve_kernel(pieces_ref, noise_ref, out_ref, aug_s, done_s, inverse_s):
    scale = 1.0 / 256.0

    def packed(r):
        at = slice(128 * r, 128 * r + 128)
        return jnp.concatenate(
            [pieces_ref[v, :, at] for v in range(8)], axis=0
        ) * scale

    corner = jnp.concatenate([packed(r) for r in range(8)], axis=0)
    mixed = jnp.concatenate([packed(r) for r in range(8, 16)], axis=0)
    extra = packed(16)
    flipped = mixed.T
    low = iota((128, 128), 0) - iota((128, 128), 1)
    first = jnp.where(low > 0, mixed, jnp.where(low < 0, flipped, jnp.broadcast_to(extra[0:1], (128, 128))))
    second = jnp.where(low > 0, flipped, mixed)
    aug_s[0:128, 0:128] = first
    aug_s[0:128, 128:256] = corner.T
    aug_s[128:256, 0:128] = corner
    aug_s[128:256, 128:256] = second
    aug_s[:, 256:512] = jnp.where(iota((256, 256), 0) == iota((256, 256), 1), 1.0, 0.0)
    inverse_s[...] = jnp.zeros((256, 256), F32)
    lane = iota((64, 128), 1)
    unit = jnp.where(iota((64, 128), 0) + 64 == lane, 1.0, 0.0)
    for s in range(4):
        top, tile = 64 * s, 128 * (s // 2)
        block = aug_s[top : top + 64, tile : tile + 128]
        if s % 2:
            block = pltpu.roll(block, 64, 1)
        block = jnp.where(lane < 64, block, unit)
        factor_block([block[8 * t : 8 * t + 8] for t in range(8)], done_s)
        inv = pltpu.roll(done_s[...], 64, 1)[:, 0:64]
        wide = 128 * (s // 2 + 1)
        inverse = exact_dot(inv, aug_s[top : top + 64, 256 : 256 + wide], ((1,), (0,)))
        inverse_s[top : top + 64, 0:wide] = inverse
        if s < 3:
            begin = 128 * ((s + 1) // 2)
            upper = exact_dot(inv, aug_s[top : top + 64, begin:256], ((1,), (0,)))
            lower = upper.T[top + 64 - begin :]
            rest = slice(top + 64, 256)
            aug_s[rest, begin:256] = aug_s[rest, begin:256] - exact_dot(lower, upper, ((1,), (0,)))
            aug_s[rest, 256 : 256 + wide] = aug_s[rest, 256 : 256 + wide] - exact_dot(
                lower, inverse, ((1,), (0,))
            )
    info = jnp.concatenate([extra[1:2], extra[2:3]], axis=1)
    inverse = inverse_s[...]
    forward = jnp.sum(inverse * info, axis=1, keepdims=True)
    out_ref[...] = exact_dot(inverse.T, noise_ref[...] + forward, ((1,), (0,)))


def draw_samples(pieces, noise):
    return pl.pallas_call(
        solve_kernel,
        out_shape=jax.ShapeDtypeStruct((256, 256), F32),
        scratch_shapes=[
            pltpu.VMEM((256, 512), F32),
            pltpu.VMEM((64, 128), F32),
            pltpu.VMEM((256, 256), F32),
        ],
        name="solve",
    )(pieces, noise)


def from_everyone(v, axes, n):
    return lax.all_to_all(jnp.broadcast_to(v[None], (n, *v.shape)), axes, 0, 0, tiled=True)


def per_device(points, inverse_cov, targets, queries, prior_precision, batch_order, noise):
    mine = jnp.concatenate([queries.reshape(-1), prior_precision])
    core = lax.axis_index("c")[None]
    mine, core = lax.optimization_barrier((mine, core))
    table = from_everyone(mine, ("z", "c"), 16)
    table = from_everyone(table, ("yh", "yl", "x"), 16).reshape(256, 144)
    own, other = expert_terms(core, batch_order, table, points, inverse_cov, targets)
    own = own + lax.ppermute(other, "c", [(0, 1), (1, 0)])
    part = lax.all_to_all(own.reshape(8, 272, 128), ("yh", "x"), 0, 0, tiled=True).sum(0)
    part = jnp.swapaxes(part.reshape(2, 8, 2176), 0, 1)
    part = jnp.broadcast_to(part[None], (2, 8, 2, 2176)).reshape(16, 2, 2176)
    part = lax.all_to_all(part, ("yl", "z"), 0, 0, tiled=True).sum(0)
    pieces = from_everyone(part, ("c", "x"), 8)
    return draw_samples(pieces, noise)


def solution(mesh):
    finer = Mesh(mesh.devices.reshape(2, 8, 2, 4, 2), AXES)
    in_specs = (
        P(AXES, None, None),
        P(AXES, None, None),
        P(AXES, None),
        P(None, AXES),
        P(AXES),
        P(),
        P(GROUP, MEMBER),
    )
    return jax.shard_map(
        per_device, mesh=finer, in_specs=in_specs, out_specs=P(GROUP, MEMBER), check_vma=False
    )
```

```python
import jax
import jax.numpy as jnp
from jax import lax
from jax.experimental import pallas as pl
from jax.experimental.pallas import tpu as pltpu
from jax.sharding import Mesh
from jax.sharding import PartitionSpec as P

AXES = ("yh", "z", "yl", "x", "c")
GROUP = ("yh", "z")
MEMBER = ("yl", "x", "c")
RATE = 0.25
EXPERT_VMEM = 60 << 20
F32, BF16 = jnp.float32, jnp.bfloat16


def iota(shape, dim):
    return lax.broadcasted_iota(jnp.int32, shape, dim)


def dot(a, b, dims):
    return lax.dot_general(a, b, (dims, ((), ())), preferred_element_type=F32)


def three_parts(v):
    a = v.astype(BF16).astype(F32)
    b = (v - a).astype(BF16).astype(F32)
    return a, b, (v - a - b)


def expert_kernel(me_ref, order_ref, table_ref, points_hbm, inv_hbm, targets_hbm, own_ref, other_ref,
                  parts_s, fold_s, points_s, cross0_s, cross1_s, proj0_s, proj1_s, left_s, prior_s,
                  inv_s, raw_s, target_s, sem):
    copies = [
        pltpu.make_async_copy(inv_hbm.at[0], inv_s, sem.at[0]),
        pltpu.make_async_copy(points_hbm.at[0], raw_s, sem.at[1]),
        pltpu.make_async_copy(targets_hbm, target_s, sem.at[2]),
    ]
    for c in copies:
        c.start()
    core = me_ref[0]
    cross, proj = (cross0_s, cross1_s), (proj0_s, proj1_s)

    def pick(n, carry):
        o = order_ref[pl.ds(pl.multiple_of(n * 1024, 1024), 1024)].reshape(1, 1024)
        hi = lax.shift_right_logical(o, 4)
        row = (hi & 128) | ((hi & 14) << 3) | (lax.shift_right_logical(hi, 3) & 14) | (hi & 1)
        hot = jnp.where(iota((256, 1024), 0) == row, 1.0, 0.0).astype(BF16)
        picked = dot(parts_s[...], hot, ((1,), (0,)))
        picked = jnp.where((iota((432, 1024), 0) & 15) == (o & 15), picked, 0.0).astype(BF16)
        q = dot(fold_s[...], picked, ((1,), (0,)))
        h, m, l = q[0:8], q[8:16], q[16:24]
        full = (h + m) + l
        norm = -RATE * jnp.sum(full * full, axis=0, keepdims=True)
        tail = jnp.concatenate([*three_parts(norm), jnp.ones((3, 1024), F32), jnp.zeros((2, 1024), F32)], axis=0)
        stacked = jnp.concatenate([h, h, h, m, m, m, l, l, l, tail], axis=0)
        left_s[pl.ds(pl.multiple_of(n * 1024, 1024), 1024), :] = stacked.T.astype(BF16)
        prior_s[pl.ds(n, 1), :] = (q[24:25] + q[25:26]) + q[26:27]
        return carry

    def kernel_columns(b, slot, j):
        at = slice(256 * j, 256 * j + 256)
        for k in range(2):
            rows = left_s[pl.ds(pl.multiple_of((b + k) * 256, 256), 256), :]
            power = dot(rows, points_s[:, at], ((1,), (0,)))
            cross[slot][272 * k : 272 * k + 256, at] = jnp.exp(power).astype(BF16)

    def write(b, terms, info, prior):
        low = iota((128, 128), 0) - iota((128, 128), 1)
        first = terms[0:128, 0:128]
        second = terms[128:256, 128:256] + jnp.where(low == 0, prior[:, 128:256], 0.0)
        mixed = jnp.where(low > 0, first, second)
        diag = jnp.sum(jnp.where(low == 0, first, 0.0), axis=0, keepdims=True) + prior[:, 0:128]
        extra = jnp.concatenate([diag, info[:, 0:128], info[:, 128:256], jnp.zeros((13, 128), F32)], axis=0)
        start = (b // 8) * 1088 + (b % 8) * 17
        for r in range(17):
            if r < 8:
                rows = terms[128 + 16 * r : 144 + 16 * r, 0:128]
            elif r < 16:
                rows = mixed[16 * (r - 8) : 16 * (r - 7), :]
            else:
                rows = extra
            a, c = rows[0:8], rows[8:16]
            own_ref[pl.ds(start + r, 8, stride=136), :] = jnp.where(core == 0, a, c)
            other_ref[pl.ds(start + r, 8, stride=136), :] = jnp.where(core == 0, c, a)

    def precision(b, slot):
        for k in range(2):
            terms = dot(
                cross[slot][256 * k : 256 * k + 272, :], proj[slot][272 * k : 272 * k + 256, :], ((1,), (1,))
            )
            prior = prior_s[pl.ds(b // 4, 1), :]
            at = 512 * slot + 256 * k
            info = terms[256:257] if k == 0 else terms[0:1]
            write(b + k, terms[16 * k : 16 * k + 256], info, prior[:, at : at + 256])

    def main(b, slot, before, after):
        for j in range(4):
            at = slice(256 * j, 256 * j + 256)
            proj[slot][:, at] = dot(cross[slot][...], inv_s[:, at], ((1,), (0,))).astype(BF16)
            if j == 0:
                precision(before, 1 - slot)
            kernel_columns(after, 1 - slot, j)

    parts_s[0:384, :] = jnp.concatenate(three_parts(table_ref[:, 0:128].T), axis=0).astype(BF16)
    parts_s[384:432, :] = jnp.concatenate(three_parts(table_ref[:, 128:144].T), axis=0).astype(BF16)
    fold_s[...] = (iota((32, 432), 1) // 16 == iota((32, 432), 0)).astype(F32).astype(BF16)
    lax.fori_loop(0, 4, pick, 0)
    copies[1].wait()
    p = raw_s[...]
    norm = -RATE * jnp.sum(p * p, axis=0, keepdims=True)
    h, m, l = three_parts(2.0 * RATE * p)
    one = jnp.ones((3, p.shape[1]), F32)
    tail = jnp.concatenate([one, *three_parts(norm), jnp.zeros((2, p.shape[1]), F32)], axis=0)
    points_s[...] = jnp.concatenate([h, m, l, h, m, l, h, m, l, tail], axis=0).astype(BF16)
    copies[2].wait()
    goal = jnp.where(
        iota((16, 1024), 0) == 0, jnp.broadcast_to(target_s[...].astype(F32), (16, 1024)), 0.0
    ).astype(BF16)
    cross0_s[256:272, :] = goal
    cross1_s[256:272, :] = goal
    for j in range(4):
        kernel_columns(0, 0, j)
    copies[0].wait()

    def step(i, carry):
        b = 4 * i
        main(b, 0, jnp.maximum(b - 2, 0), b + 2)
        main(b + 2, 1, b, jnp.minimum(b + 4, 14))
        return carry

    lax.fori_loop(0, 4, step, 0)
    precision(14, 1)


def expert_terms(core, order, table, points, inverse_cov, targets):
    vmem = pl.BlockSpec(memory_space=pltpu.VMEM)
    hbm = pl.BlockSpec(memory_space=pltpu.HBM)
    return pl.pallas_call(
        expert_kernel,
        out_shape=(jax.ShapeDtypeStruct((2176, 128), F32),) * 2,
        in_specs=[pl.BlockSpec(memory_space=pltpu.SMEM), vmem, vmem, hbm, hbm, hbm],
        out_specs=(vmem, vmem),
        scratch_shapes=[
            pltpu.VMEM((432, 256), BF16),
            pltpu.VMEM((32, 432), BF16),
            pltpu.VMEM((80, 1024), BF16),
            pltpu.VMEM((528, 1024), BF16),
            pltpu.VMEM((528, 1024), BF16),
            pltpu.VMEM((528, 1024), BF16),
            pltpu.VMEM((528, 1024), BF16),
            pltpu.VMEM((4096, 80), BF16),
            pltpu.VMEM((8, 1024), F32),
            pltpu.VMEM((1024, 1024), BF16),
            pltpu.VMEM((8, 1024), F32),
            pltpu.VMEM((1, 1024), BF16),
            pltpu.SemaphoreType.DMA((3,)),
        ],
        compiler_params=pltpu.CompilerParams(vmem_limit_bytes=EXPERT_VMEM),
        name="expert",
    )(core, order, table, points, inverse_cov, targets)


def exact_dot(a, b, dims):
    return lax.dot_general(
        a, b, (dims, ((), ())), precision=lax.Precision.HIGHEST, preferred_element_type=F32
    )


def along_lanes(v, i):
    return jnp.broadcast_to(v[:, i : i + 1], (8, 128))


def along_rows(v, i):
    return jnp.broadcast_to(v[i : i + 1, :], (8, 128))


def factor_block(groups, done_ref):
    for p in range(8):
        g = groups[p]
        rows = [along_rows(g, i) for i in range(8)]
        b = [[along_lanes(rows[i], 8 * p + j) for j in range(i + 1)] for i in range(8)]
        ahead = [[along_lanes(groups[t], 8 * p + j) for j in range(8)] for t in range(p + 1, 8)]
        for k in range(8):
            r = lax.rsqrt(b[k][k])
            for i in range(k + 1, 8):
                b[i][k] = b[i][k] * r
            for i in range(k + 1, 8):
                for j in range(k + 1, i + 1):
                    b[i][j] = b[i][j] - b[i][k] * b[j][k]
            rows[k] = rows[k] * r
            for i in range(k + 1, 8):
                rows[i] = rows[i] - b[i][k] * rows[k]
            for t in range(p + 1, 8):
                c = ahead[t - p - 1]
                c[k] = c[k] * r
                for j in range(k + 1, 8):
                    c[j] = c[j] - c[k] * b[j][k]
                groups[t] = groups[t] - c[k] * rows[k]
            done_ref[8 * p + k : 8 * p + k + 1, :] = rows[k][0:1]


def solve_kernel(pieces_ref, noise_ref, out_ref, aug_s, done_s, inverse_s):
    def packed(r):
        at = slice(128 * r, 128 * r + 128)
        return jnp.concatenate(
            [pieces_ref[v, :, at] for v in range(8)], axis=0
        )

    corner = jnp.concatenate([packed(r) for r in range(8)], axis=0)
    mixed = jnp.concatenate([packed(r) for r in range(8, 16)], axis=0)
    extra = packed(16)
    flipped = mixed.T
    low = iota((128, 128), 0) - iota((128, 128), 1)
    first = jnp.where(low > 0, mixed, jnp.where(low < 0, flipped, jnp.broadcast_to(extra[0:1], (128, 128))))
    second = jnp.where(low > 0, flipped, mixed)
    aug_s[0:128, 0:128] = first
    aug_s[0:128, 128:256] = corner.T
    aug_s[128:256, 0:128] = corner
    aug_s[128:256, 128:256] = second
    aug_s[:, 256:512] = jnp.where(iota((256, 256), 0) == iota((256, 256), 1), 1.0, 0.0)
    inverse_s[...] = jnp.zeros((256, 256), F32)
    lane = iota((64, 128), 1)
    unit = jnp.where(iota((64, 128), 0) + 64 == lane, 1.0, 0.0)
    for s in range(4):
        top, tile = 64 * s, 128 * (s // 2)
        block = aug_s[top : top + 64, tile : tile + 128]
        if s % 2:
            block = pltpu.roll(block, 64, 1)
        block = jnp.where(lane < 64, block, unit)
        factor_block([block[8 * t : 8 * t + 8] for t in range(8)], done_s)
        inv = pltpu.roll(done_s[...], 64, 1)[:, 0:64]
        wide = 128 * (s // 2 + 1)
        inverse = exact_dot(inv, aug_s[top : top + 64, 256 : 256 + wide], ((1,), (0,)))
        inverse_s[top : top + 64, 0:wide] = inverse
        if s < 3:
            begin = 128 * ((s + 1) // 2)
            upper = exact_dot(inv, aug_s[top : top + 64, begin:256], ((1,), (0,)))
            lower = upper.T[top + 64 - begin :]
            rest = slice(top + 64, 256)
            aug_s[rest, begin:256] = aug_s[rest, begin:256] - exact_dot(lower, upper, ((1,), (0,)))
            aug_s[rest, 256 : 256 + wide] = aug_s[rest, 256 : 256 + wide] - exact_dot(
                lower, inverse, ((1,), (0,))
            )
    info = jnp.concatenate([extra[1:2], extra[2:3]], axis=1)
    inverse = inverse_s[...]
    forward = jnp.sum(inverse * info, axis=1, keepdims=True)
    out_ref[...] = exact_dot(inverse.T, noise_ref[...] + forward, ((1,), (0,)))


def draw_samples(pieces, noise):
    return pl.pallas_call(
        solve_kernel,
        out_shape=jax.ShapeDtypeStruct((256, 256), F32),
        scratch_shapes=[
            pltpu.VMEM((256, 512), F32),
            pltpu.VMEM((64, 128), F32),
            pltpu.VMEM((256, 256), F32),
        ],
        name="solve",
    )(pieces, noise)


def from_everyone(v, axes, n):
    return lax.all_to_all(jnp.broadcast_to(v[None], (n, *v.shape)), axes, 0, 0, tiled=True)


def per_device(points, inverse_cov, targets, queries, prior_precision, batch_order, noise):
    mine = lax.optimization_barrier(jnp.concatenate([queries, prior_precision[None]], axis=0)).reshape(-1)
    core = lax.axis_index("c")[None]
    mine, core = lax.optimization_barrier((mine, core))
    table = from_everyone(mine, ("z", "c"), 16)
    table = from_everyone(table, ("yh", "yl", "x"), 16).reshape(256, 144)
    own, other = expert_terms(core, batch_order, table, points, inverse_cov, targets)
    scale = 1.0 / 256.0
    theirs = lax.ppermute(other, "c", [(0, 1), (1, 0)])
    own = lax.optimization_barrier(own * scale) + theirs * scale
    part = lax.all_to_all(own.reshape(8, 272, 128), ("yh", "x"), 0, 0, tiled=True).sum(0)
    part = jnp.swapaxes(part.reshape(2, 8, 2176), 0, 1)
    part = jnp.broadcast_to(part[None], (2, 8, 2, 2176)).reshape(16, 2, 2176)
    part = lax.all_to_all(part, ("yl", "z"), 0, 0, tiled=True).sum(0)
    pieces = from_everyone(part, ("c", "x"), 8)
    return draw_samples(pieces, noise)


def solution(mesh):
    finer = Mesh(mesh.devices.reshape(2, 8, 2, 4, 2), AXES)
    in_specs = (
        P(AXES, None, None),
        P(AXES, None, None),
        P(AXES, None),
        P(None, AXES),
        P(AXES),
        P(),
        P(GROUP, MEMBER),
    )
    return jax.shard_map(
        per_device, mesh=finer, in_specs=in_specs, out_specs=P(GROUP, MEMBER), check_vma=False
    )
```

```python
import jax
import jax.numpy as jnp
from jax import lax
from jax.experimental import pallas as pl
from jax.experimental.pallas import tpu as pltpu
from jax.sharding import Mesh
from jax.sharding import PartitionSpec as P

AXES = ("yh", "z", "yl", "x", "c")
GROUP = ("yh", "z")
MEMBER = ("yl", "x", "c")
RATE = 0.25
EXPERT_VMEM = 60 << 20
F32, BF16 = jnp.float32, jnp.bfloat16


def iota(shape, dim):
    return lax.broadcasted_iota(jnp.int32, shape, dim)


def dot(a, b, dims):
    return lax.dot_general(a, b, (dims, ((), ())), preferred_element_type=F32)


def three_parts(v):
    a = v.astype(BF16).astype(F32)
    b = (v - a).astype(BF16).astype(F32)
    return a, b, (v - a - b)


def expert_kernel(me_ref, order_ref, table_ref, points_hbm, inv_hbm, targets_hbm, own_ref, other_ref,
                  parts_s, fold_s, points_s, cross0_s, cross1_s, proj0_s, proj1_s, left_s, prior_s,
                  inv_s, raw_s, target_s, sem):
    copies = [
        pltpu.make_async_copy(inv_hbm.at[0], inv_s, sem.at[0]),
        pltpu.make_async_copy(points_hbm.at[0], raw_s, sem.at[1]),
        pltpu.make_async_copy(targets_hbm, target_s, sem.at[2]),
    ]
    for c in copies:
        c.start()
    core = me_ref[0]
    cross, proj = (cross0_s, cross1_s), (proj0_s, proj1_s)

    def pick(n, carry):
        o = order_ref[pl.ds(pl.multiple_of(n * 1024, 1024), 1024)].reshape(1, 1024)
        hi = lax.shift_right_logical(o, 4)
        row = (hi & 128) | ((hi & 14) << 3) | (lax.shift_right_logical(hi, 3) & 14) | (hi & 1)
        hot = jnp.where(iota((256, 1024), 0) == row, 1.0, 0.0).astype(BF16)
        picked = dot(parts_s[...], hot, ((1,), (0,)))
        picked = jnp.where((iota((432, 1024), 0) & 15) == (o & 15), picked, 0.0).astype(BF16)
        q = dot(fold_s[...], picked, ((1,), (0,)))
        h, m, l = q[0:8], q[8:16], q[16:24]
        full = (h + m) + l
        norm = -RATE * jnp.sum(full * full, axis=0, keepdims=True)
        tail = jnp.concatenate([*three_parts(norm), jnp.ones((3, 1024), F32), jnp.zeros((2, 1024), F32)], axis=0)
        stacked = jnp.concatenate([h, h, h, m, m, m, l, l, l, tail], axis=0)
        left_s[pl.ds(pl.multiple_of(n * 1024, 1024), 1024), :] = stacked.T.astype(BF16)
        prior_s[pl.ds(n, 1), :] = (q[24:25] + q[25:26]) + q[26:27]
        return carry

    def kernel_columns(b, slot, j):
        at = slice(256 * j, 256 * j + 256)
        for k in range(2):
            rows = left_s[pl.ds(pl.multiple_of((b + k) * 256, 256), 256), :]
            power = dot(rows, points_s[:, at], ((1,), (0,)))
            cross[slot][272 * k : 272 * k + 256, at] = jnp.exp(power).astype(BF16)

    def write(b, terms, info, prior):
        low = iota((128, 128), 0) - iota((128, 128), 1)
        first = terms[0:128, 0:128]
        second = terms[128:256, 128:256] + jnp.where(low == 0, prior[:, 128:256], 0.0)
        mixed = jnp.where(low > 0, first, second)
        diag = jnp.sum(jnp.where(low == 0, first, 0.0), axis=0, keepdims=True) + prior[:, 0:128]
        extra = jnp.concatenate([diag, info[:, 0:128], info[:, 128:256], jnp.zeros((13, 128), F32)], axis=0)
        start = (b // 8) * 1088 + (b % 8) * 17
        for r in range(17):
            if r < 8:
                rows = terms[128 + 16 * r : 144 + 16 * r, 0:128]
            elif r < 16:
                rows = mixed[16 * (r - 8) : 16 * (r - 7), :]
            else:
                rows = extra
            a, c = rows[0:8], rows[8:16]
            own_ref[pl.ds(start + r, 8, stride=136), :] = jnp.where(core == 0, a, c)
            other_ref[pl.ds(start + r, 8, stride=136), :] = jnp.where(core == 0, c, a)

    def precision(b, slot):
        for k in range(2):
            terms = dot(
                cross[slot][256 * k : 256 * k + 272, :], proj[slot][272 * k : 272 * k + 256, :], ((1,), (1,))
            )
            prior = prior_s[pl.ds(b // 4, 1), :]
            at = 512 * slot + 256 * k
            info = terms[256:257] if k == 0 else terms[0:1]
            write(b + k, terms[16 * k : 16 * k + 256], info, prior[:, at : at + 256])

    def main(b, slot, before, after):
        for j in range(4):
            at = slice(256 * j, 256 * j + 256)
            proj[slot][:, at] = dot(cross[slot][...], inv_s[:, at], ((1,), (0,))).astype(BF16)
            if j == 0:
                precision(before, 1 - slot)
            kernel_columns(after, 1 - slot, j)

    parts_s[0:384, :] = jnp.concatenate(three_parts(table_ref[:, 0:128].T), axis=0).astype(BF16)
    parts_s[384:432, :] = jnp.concatenate(three_parts(table_ref[:, 128:144].T), axis=0).astype(BF16)
    fold_s[...] = (iota((32, 432), 1) // 16 == iota((32, 432), 0)).astype(F32).astype(BF16)
    lax.fori_loop(0, 4, pick, 0)
    copies[1].wait()
    p = raw_s[...]
    norm = -RATE * jnp.sum(p * p, axis=0, keepdims=True)
    h, m, l = three_parts(2.0 * RATE * p)
    one = jnp.ones((3, p.shape[1]), F32)
    tail = jnp.concatenate([one, *three_parts(norm), jnp.zeros((2, p.shape[1]), F32)], axis=0)
    points_s[...] = jnp.concatenate([h, m, l, h, m, l, h, m, l, tail], axis=0).astype(BF16)
    copies[2].wait()
    goal = jnp.where(
        iota((16, 1024), 0) == 0, jnp.broadcast_to(target_s[...].astype(F32), (16, 1024)), 0.0
    ).astype(BF16)
    cross0_s[256:272, :] = goal
    cross1_s[256:272, :] = goal
    for j in range(4):
        kernel_columns(0, 0, j)
    copies[0].wait()

    def step(i, carry):
        b = 4 * i
        main(b, 0, jnp.maximum(b - 2, 0), b + 2)
        main(b + 2, 1, b, jnp.minimum(b + 4, 14))
        return carry

    lax.fori_loop(0, 4, step, 0)
    precision(14, 1)


def expert_terms(core, order, table, points, inverse_cov, targets):
    vmem = pl.BlockSpec(memory_space=pltpu.VMEM)
    hbm = pl.BlockSpec(memory_space=pltpu.HBM)
    return pl.pallas_call(
        expert_kernel,
        out_shape=(jax.ShapeDtypeStruct((2176, 128), F32),) * 2,
        in_specs=[pl.BlockSpec(memory_space=pltpu.SMEM), vmem, vmem, hbm, hbm, hbm],
        out_specs=(vmem, vmem),
        scratch_shapes=[
            pltpu.VMEM((432, 256), BF16),
            pltpu.VMEM((32, 432), BF16),
            pltpu.VMEM((80, 1024), BF16),
            pltpu.VMEM((528, 1024), BF16),
            pltpu.VMEM((528, 1024), BF16),
            pltpu.VMEM((528, 1024), BF16),
            pltpu.VMEM((528, 1024), BF16),
            pltpu.VMEM((4096, 80), BF16),
            pltpu.VMEM((8, 1024), F32),
            pltpu.VMEM((1024, 1024), BF16),
            pltpu.VMEM((8, 1024), F32),
            pltpu.VMEM((1, 1024), BF16),
            pltpu.SemaphoreType.DMA((3,)),
        ],
        compiler_params=pltpu.CompilerParams(vmem_limit_bytes=EXPERT_VMEM),
        name="expert",
    )(core, order, table, points, inverse_cov, targets)


def exact_dot(a, b, dims):
    return lax.dot_general(
        a, b, (dims, ((), ())), precision=lax.Precision.HIGHEST, preferred_element_type=F32
    )


def along_lanes(v, i):
    return jnp.broadcast_to(v[:, i : i + 1], (8, 128))


def factor_block(groups, done_ref, splat_ref):
    for p in range(8):
        g = groups[p]
        at = 72 * p
        for j in range(8):
            splat_ref[at + 8 * j : at + 8 * j + 8, :] = along_lanes(g, 8 * p + j)
        splat_ref[at + 64 : at + 72, :] = g
        b = [[splat_ref[pl.ds(at + 8 * j + i, 8, stride=0), :] for j in range(i + 1)] for i in range(8)]
        rows = [splat_ref[pl.ds(at + 64 + i, 8, stride=0), :] for i in range(8)]
        ahead = [[along_lanes(groups[t], 8 * p + j) for j in range(8)] for t in range(p + 1, 8)]
        for k in range(8):
            r = lax.rsqrt(b[k][k])
            for i in range(k + 1, 8):
                b[i][k] = b[i][k] * r
            for i in range(k + 1, 8):
                for j in range(k + 1, i + 1):
                    b[i][j] = b[i][j] - b[i][k] * b[j][k]
            rows[k] = rows[k] * r
            for i in range(k + 1, 8):
                rows[i] = rows[i] - b[i][k] * rows[k]
            for t in range(p + 1, 8):
                c = ahead[t - p - 1]
                c[k] = c[k] * r
                for j in range(k + 1, 8):
                    c[j] = c[j] - c[k] * b[j][k]
                groups[t] = groups[t] - c[k] * rows[k]
            done_ref[8 * p + k : 8 * p + k + 1, :] = rows[k][0:1]


def solve_kernel(pieces_ref, noise_ref, out_ref, aug_s, done_s, inverse_s, splat_s):
    def packed(r):
        at = slice(128 * r, 128 * r + 128)
        return jnp.concatenate(
            [pieces_ref[v, :, at] for v in range(8)], axis=0
        )

    corner = jnp.concatenate([packed(r) for r in range(8)], axis=0)
    mixed = jnp.concatenate([packed(r) for r in range(8, 16)], axis=0)
    extra = packed(16)
    flipped = mixed.T
    low = iota((128, 128), 0) - iota((128, 128), 1)
    first = jnp.where(low > 0, mixed, jnp.where(low < 0, flipped, jnp.broadcast_to(extra[0:1], (128, 128))))
    second = jnp.where(low > 0, flipped, mixed)
    aug_s[0:128, 0:128] = first
    aug_s[0:128, 128:256] = corner.T
    aug_s[128:256, 0:128] = corner
    aug_s[128:256, 128:256] = second
    aug_s[:, 256:512] = jnp.where(iota((256, 256), 0) == iota((256, 256), 1), 1.0, 0.0)
    inverse_s[...] = jnp.zeros((256, 256), F32)
    lane = iota((64, 128), 1)
    unit = jnp.where(iota((64, 128), 0) + 64 == lane, 1.0, 0.0)
    for s in range(4):
        top, tile = 64 * s, 128 * (s // 2)
        block = aug_s[top : top + 64, tile : tile + 128]
        if s % 2:
            block = pltpu.roll(block, 64, 1)
        block = jnp.where(lane < 64, block, unit)
        factor_block([block[8 * t : 8 * t + 8] for t in range(8)], done_s, splat_s)
        inv = pltpu.roll(done_s[...], 64, 1)[:, 0:64]
        wide = 128 * (s // 2 + 1)
        inverse = exact_dot(inv, aug_s[top : top + 64, 256 : 256 + wide], ((1,), (0,)))
        inverse_s[top : top + 64, 0:wide] = inverse
        if s < 3:
            begin = 128 * ((s + 1) // 2)
            upper = exact_dot(inv, aug_s[top : top + 64, begin:256], ((1,), (0,)))
            lower = upper.T[top + 64 - begin :]
            rest = slice(top + 64, 256)
            aug_s[rest, begin:256] = aug_s[rest, begin:256] - exact_dot(lower, upper, ((1,), (0,)))
            aug_s[rest, 256 : 256 + wide] = aug_s[rest, 256 : 256 + wide] - exact_dot(
                lower, inverse, ((1,), (0,))
            )
    info = jnp.concatenate([extra[1:2], extra[2:3]], axis=1)
    inverse = inverse_s[...]
    forward = jnp.sum(inverse * info, axis=1, keepdims=True)
    out_ref[...] = exact_dot(inverse.T, noise_ref[...] + forward, ((1,), (0,)))


def draw_samples(pieces, noise):
    return pl.pallas_call(
        solve_kernel,
        out_shape=jax.ShapeDtypeStruct((256, 256), F32),
        scratch_shapes=[
            pltpu.VMEM((256, 512), F32),
            pltpu.VMEM((64, 128), F32),
            pltpu.VMEM((256, 256), F32),
            pltpu.VMEM((584, 128), F32),
        ],
        name="solve",
    )(pieces, noise)


def from_everyone(v, axes, n):
    return lax.all_to_all(jnp.broadcast_to(v[None], (n, *v.shape)), axes, 0, 0, tiled=True)


def per_device(points, inverse_cov, targets, queries, prior_precision, batch_order, noise):
    mine = lax.optimization_barrier(jnp.concatenate([queries, prior_precision[None]], axis=0)).reshape(-1)
    core = lax.axis_index("c")[None]
    mine, core = lax.optimization_barrier((mine, core))
    table = from_everyone(mine, ("z", "c"), 16)
    table = from_everyone(table, ("yh", "yl", "x"), 16).reshape(256, 144)
    own, other = expert_terms(core, batch_order, table, points, inverse_cov, targets)
    scale = 1.0 / 256.0
    theirs = lax.ppermute(other, "c", [(0, 1), (1, 0)])
    own = lax.optimization_barrier(own * scale) + theirs * scale
    part = lax.all_to_all(own.reshape(8, 272, 128), ("yh", "x"), 0, 0, tiled=True).sum(0)
    part = jnp.swapaxes(part.reshape(2, 8, 2176), 0, 1)
    part = jnp.broadcast_to(part[None], (2, 8, 2, 2176)).reshape(16, 2, 2176)
    part = lax.all_to_all(part, ("yl", "z"), 0, 0, tiled=True).sum(0)
    pieces = from_everyone(part, ("c", "x"), 8)
    return draw_samples(pieces, noise)


def solution(mesh):
    finer = Mesh(mesh.devices.reshape(2, 8, 2, 4, 2), AXES)
    in_specs = (
        P(AXES, None, None),
        P(AXES, None, None),
        P(AXES, None),
        P(None, AXES),
        P(AXES),
        P(),
        P(GROUP, MEMBER),
    )
    return jax.shard_map(
        per_device, mesh=finer, in_specs=in_specs, out_specs=P(GROUP, MEMBER), check_vma=False
    )
```
